32 devices in a mesh: grp: 2 (over y), frm: 4 (over z), row: 2 (over x), sub: 2 (over core).
Axes of the slice: x: 2, y: 2, z: 4, core: 2. Of those that a mesh axis runs over, the one named last changes fastest.
Arguments:
- signal: bfloat16 [64, 65536], P('row', ('grp', 'frm', 'sub')), parts along dimension 1, may hold values from -6 to 6
- w_start: float32 [2560, 32], P('row'), may hold values from 0.02 to 0.4
- h_start: float32 [32, 65536], P(None, ('grp', 'frm', 'sub')), parts along dimension 1, may hold values from 0.02 to 0.4
Outputs:
- synergies: float32 [5120, 32], P(('grp', 'row')), parts along dimension 0
- activations: float32 [32, 65536], P(None, ('grp', 'frm', 'sub')), parts along dimension 1
The draws below stay inside these ranges and needn't reach their ends.
There are 2 independent parts, one for each index of `grp`. The reference program is written for one: setup_inputs(seed, part) draws one part's arguments, and reference() takes and returns one part's arrays. A program takes and returns all parts, laid end to end along the dimension named above; an argument that names none is the same for every part. Nothing has to cross between parts.
All inputs are finite; a program needn't handle non-finite values.
Results may differ from the reference program's by a relative error of at most 0.0019.
Values may be sent and summed in bfloat16 or wider, within the bound.
A program may use at most 128 MiB of HBM per device.

```python
import math
import jax
import jax.numpy as jnp
from jax import lax

C = 64
NF = 40
RANK = 32
TAPS = 128
ITERS = 2
FR_DEV = 4096
FRAMES = 32768
ROWS = 2560


def shard_levels(key, extent, split, least, largest):
    factor_of, own = 1.0, jax.random.fold_in(key, 6)
    for axis_at, blocks in split:
        steps = jnp.exp(jax.random.uniform(jax.random.fold_in(own, axis_at), (blocks,), jnp.float32, least / len(split), largest / len(split)))
        factor_of = factor_of * jnp.repeat(steps, extent[axis_at] // blocks).reshape([-1 if axis == axis_at else 1 for axis in range(len(extent))])
    return factor_of


def noise(own_key, extent, spread, reach, shards=(), kind=jnp.bfloat16):
    result = spread * jax.random.normal(own_key, extent, jnp.float32)
    if shards:
        result = result * shard_levels(own_key, extent, shards, -0.22, 0.18)
    return jnp.clip(result, -reach, reach).astype(kind)


def setup_inputs(seed: int = 0, part: int = 0) -> dict:
    arg_keys = jax.random.split(jax.random.key(seed), 4)
    part_keys = jax.random.split(jax.random.fold_in(arg_keys[3], part), 4)
    return {
        "signal": noise(part_keys[0], (C, FRAMES), 1.0, 6.0, ((0, 2), (1, 8))),
        "w_start": jnp.clip(jnp.exp(math.log(0.4) - 2.9957323 * jax.random.uniform(arg_keys[1], (ROWS, RANK), jnp.float32) ** shard_levels(arg_keys[1], (ROWS, RANK), ((0, 2),), -0.2, 0.2)), 0.02, 0.4),
        "h_start": jnp.clip(jnp.exp(math.log(0.4) - 2.9957323 * jax.random.uniform(part_keys[2], (RANK, FRAMES), jnp.float32) ** shard_levels(part_keys[2], (RANK, FRAMES), ((1, 8),), -0.2, 0.2)), 0.02, 0.4),
    }


def morlet(offsets):
    level = jnp.arange(NF, dtype=jnp.float32) / (NF - 1)
    freq = 2.0 * jnp.power(12.0, level)
    sigma = 7.0 / (2.0 * math.pi * freq)
    all_times = (jnp.arange(TAPS, dtype=jnp.float32) - TAPS // 2) / 50.0
    all_env = jnp.exp(-all_times[None, :] ** 2 / (2.0 * sigma[:, None] ** 2))
    scale = 1.0 / jnp.sqrt(lax.optimization_barrier(jnp.sum(all_env * all_env, axis=1)))
    extra = (1,) * offsets.ndim
    freq_b = freq.reshape((NF,) + extra)
    sigma_b = sigma.reshape((NF,) + extra)
    scale_b = scale.reshape((NF,) + extra)
    times = (offsets - TAPS // 2) / 50.0
    env = jnp.exp(-times ** 2 / (2.0 * sigma_b ** 2)) * scale_b
    phase = 2.0 * math.pi * freq_b * times
    return jnp.stack([env * jnp.cos(phase), env * jnp.sin(phase)])

def reference(signal, w_start, h_start):
    kernel = morlet(jnp.arange(TAPS, dtype=jnp.float32)).astype(jnp.bfloat16)
    kernel_f = kernel.astype(jnp.float32)
    half_span = TAPS // 2
    padded = jnp.pad(signal, ((0, 0), (half_span, half_span)))
    nblocks = FRAMES // FR_DEV
    window_idx = jnp.arange(FR_DEV, dtype=jnp.int32)[:, None] + jnp.arange(TAPS, dtype=jnp.int32)[None, :]
    high = lax.Precision.HIGHEST

    def spectra_block(index):
        segment = lax.dynamic_slice_in_dim(padded, (index * FR_DEV).astype(jnp.int32), FR_DEV + TAPS, 1)
        windows = segment[:, window_idx].astype(jnp.float32)
        coeffs = jnp.einsum('ctk,pfk->cpft', windows, kernel_f)
        power_grid = coeffs[:, 0] ** 2 + coeffs[:, 1] ** 2
        return power_grid.reshape(C * NF, FR_DEV).astype(jnp.bfloat16)
    synergies = w_start
    activations = h_start
    for update in range(ITERS):
        synergies_low = synergies.astype(jnp.bfloat16)
        gram_sum = jnp.dot(synergies.T, synergies, precision=high)

        def scan_step(carry, index):
            crossed, h_gram = carry
            spectra = spectra_block(index)
            summed = jnp.dot(synergies_low.T, spectra, preferred_element_type=jnp.float32)
            old_block = lax.dynamic_slice_in_dim(activations, (index * FR_DEV).astype(jnp.int32), FR_DEV, 1)
            new_block = old_block * summed / jnp.dot(gram_sum, old_block, precision=high)
            block_low = new_block.astype(jnp.bfloat16)
            crossed = crossed + jnp.dot(spectra, block_low.T, preferred_element_type=jnp.float32)
            h_gram = h_gram + jnp.dot(new_block, new_block.T, precision=high)
            return ((crossed, h_gram), new_block)
        start_carry = (jnp.zeros((C * NF, RANK), jnp.float32), jnp.zeros((RANK, RANK), jnp.float32))
        (crossed, h_gram), new_blocks = lax.scan(scan_step, start_carry, jnp.arange(nblocks, dtype=jnp.int32))
        activations = new_blocks.transpose(1, 0, 2).reshape(RANK, FRAMES)
        synergies = synergies * crossed / jnp.dot(synergies, h_gram, precision=high)
    return (synergies, activations)
```

```python
import functools
import math

import jax
import jax.numpy as jnp
import numpy as np
from jax import lax
from jax.experimental import pallas as pl
from jax.experimental.pallas import tpu as pltpu
from jax.sharding import PartitionSpec as P

NF = 40
TAPS = 128
ITERS = 2
CHUNKS = 4
UNROLL = 4
HIGH = lax.Precision.HIGHEST
MESH = pl.DeviceIdType.MESH
F32, BF16 = jnp.float32, jnp.bfloat16
LANES = (((1,), (1,)), ((), ()))


def circulants():
    freq = 2.0 * 12.0 ** (np.arange(NF) / (NF - 1))
    sigma = 7.0 / (2.0 * math.pi * freq)
    times = (np.arange(TAPS) - TAPS // 2) / 50.0
    env = np.exp(-(times[None, :] ** 2) / (2.0 * sigma[:, None] ** 2))
    env = env / np.sqrt(np.sum(env * env, axis=1, keepdims=True))
    phase = 2.0 * math.pi * freq[:, None] * times[None, :]
    taps = np.stack([env * np.cos(phase), env * np.sin(phase)], axis=1).astype(np.float32)
    at = np.arange(TAPS)
    table = taps[:, :, (at[:, None] - at[None, :]) % TAPS]
    return table.transpose(0, 2, 1, 3).reshape(NF, TAPS, 2 * TAPS).astype(BF16)


def kernel(
    sizes,
    sig_ref, w_ref, h_ref, circ_ref,
    w_out, h_out,
    circ, table, halo, lhs, spec, sums, grams, acc, subs, parts, wt,
    circ_sem, halo_send, halo_recv, sum_send, sum_recv, gram_send, gram_recv,
    sub_send, sub_recv, part_send, part_recv, w_send, w_recv,
):
    nfrm, nrow, nsub = sizes
    frm, row, sub = lax.axis_index("frm"), lax.axis_index("row"), lax.axis_index("sub")
    channels, frames = sig_ref.shape
    rank, rows = w_ref.shape
    half = rank // nsub
    blocks = frames // TAPS
    per = blocks // CHUNKS
    wide = frames // CHUNKS
    place = frm * nsub + sub
    has_left, has_right = place > 0, place < nfrm * nsub - 1
    sent = []

    load = pltpu.make_async_copy(circ_ref, circ, circ_sem)
    load.start()

    def peer(name, step):
        size = {"frm": nfrm, "row": nrow, "sub": nsub}[name]
        return lax.rem(lax.axis_index(name) + step, size)

    def neighbour(side):
        at = place + side
        return {"frm": at // nsub, "sub": lax.rem(at, nsub)}

    grams[...] = jnp.zeros_like(grams)
    acc[...] = jnp.zeros_like(acc)
    wt[0] = w_ref[...]

    barrier = pltpu.get_barrier_semaphore()
    for name, size in (("frm", nfrm), ("row", nrow), ("sub", nsub)):
        for step in range(1, size):
            pl.semaphore_signal(barrier, inc=1, device_id={name: peer(name, step)}, device_id_type=MESH)

    @pl.when(has_left)
    def _():
        pl.semaphore_signal(barrier, inc=1, device_id=neighbour(-1), device_id_type=MESH)

    @pl.when(has_right)
    def _():
        pl.semaphore_signal(barrier, inc=1, device_id=neighbour(1), device_id_type=MESH)

    sides = has_left.astype(jnp.int32) + has_right.astype(jnp.int32)
    pl.semaphore_wait(barrier, nfrm + nrow + nsub - 3 + sides)

    def push(src, dst, send, recv, to):
        copy = pltpu.make_async_remote_copy(
            src_ref=src, dst_ref=dst, send_sem=send, recv_sem=recv, device_id=to, device_id_type=MESH
        )
        copy.start()
        sent.append(copy)
        return copy

    def edge(side):
        return pltpu.make_async_remote_copy(
            src_ref=sig_ref.at[:, pl.ds(frames - TAPS, TAPS)] if side > 0 else sig_ref.at[:, pl.ds(0, TAPS)],
            dst_ref=halo.at[0 if side > 0 else 1],
            send_sem=halo_send.at[0 if side > 0 else 1],
            recv_sem=halo_recv.at[0 if side > 0 else 1],
            device_id=neighbour(side),
            device_id_type=MESH,
        )

    @pl.when(has_right)
    def _():
        edge(1).start()

    @pl.when(has_left)
    def _():
        edge(-1).start()

    @pl.when(jnp.logical_not(has_left))
    def _():
        halo[0] = jnp.zeros((channels, TAPS), BF16)

    @pl.when(jnp.logical_not(has_right))
    def _():
        halo[1] = jnp.zeros((channels, TAPS), BF16)

    def share_gram(it):
        now = wt[it]
        grams[it, row, :, 0:rank] = lax.dot_general(now, now, LANES, precision=HIGH, preferred_element_type=F32)
        return [
            push(grams.at[it, row], grams.at[it, row], gram_send.at[it, s - 1], gram_recv.at[it, s - 1], {"row": peer("row", s)})
            for s in range(1, nrow)
        ]

    gram_copies = share_gram(0)

    load.wait()
    source = lax.broadcasted_iota(jnp.int32, (TAPS, 2 * TAPS), 0)
    target = lax.rem(lax.broadcasted_iota(jnp.int32, (TAPS, 2 * TAPS), 1), TAPS)
    lead = jnp.where(source >= target, 1.0, 0.0).astype(BF16)
    trail = jnp.where(source >= target, 0.0, 1.0).astype(BF16)

    def fill(f, carry):
        table[f, 0:TAPS, :] = circ[f] * lead
        table[f, TAPS : 2 * TAPS, :] = circ[f] * trail
        return carry

    lax.fori_loop(0, NF, fill, 0)

    @pl.when(has_left)
    def _():
        edge(1).wait_recv()

    @pl.when(has_right)
    def _():
        edge(-1).wait_recv()

    low_half = lax.broadcasted_iota(jnp.int32, (channels, TAPS), 1) < TAPS // 2
    before = pltpu.roll(halo[0].astype(F32), TAPS // 2, 1)
    for i in range(blocks + 1):
        after = sig_ref[:, i * TAPS : (i + 1) * TAPS] if i < blocks else halo[1]
        after = pltpu.roll(after.astype(F32), TAPS // 2, 1)
        piece = jnp.where(low_half, before, after).astype(BF16)
        if i < blocks:
            lhs[i * channels : (i + 1) * channels, 0:TAPS] = piece
        if i > 0:
            lhs[(i - 1) * channels : i * channels, TAPS : 2 * TAPS] = piece
        before = after

    def wavelets(q):
        first = q * per

        def group(g, carry):
            for u in range(UNROLL):
                f = g * UNROLL + u
                out = jnp.dot(
                    lhs[first * channels : (first + per) * channels, :], table[f], preferred_element_type=F32
                )
                power = (out[:, :TAPS] * out[:, :TAPS] + out[:, TAPS:] * out[:, TAPS:]).astype(BF16)
                at = pl.multiple_of(f * channels, channels)
                for b in range(per):
                    spec[pl.ds(at, channels), (first + b) * TAPS : (first + b + 1) * TAPS] = power[
                        b * channels : (b + 1) * channels
                    ]
            return carry

        lax.fori_loop(0, NF // UNROLL, group, 0)

    def project(it, q, w_low):
        sums[it, row, q] = jnp.dot(w_low, spec[:, q * wide : (q + 1) * wide], preferred_element_type=F32)
        return [
            push(
                sums.at[it, row, q], sums.at[it, row, q],
                sum_send.at[it, q, s - 1], sum_recv.at[it, q, s - 1], {"row": peer("row", s)},
            )
            for s in range(1, nrow)
        ]

    def update_h(it, q, copies, gram):
        for copy in copies:
            copy.wait_recv()
        total = sums[it, 0, q]
        for s in range(1, nrow):
            total = total + sums[it, s, q]
        cols = slice(q * wide, (q + 1) * wide)
        old = h_ref[:, cols] if it == 0 else h_out[:, cols]
        new = old * total / jnp.dot(gram, old, precision=HIGH, preferred_element_type=F32)
        h_out[:, cols] = new
        acc[it, :, 0:rows] += lax.dot_general(new.astype(BF16), spec[:, cols], LANES, preferred_element_type=F32)
        acc[it, :, rows : rows + rank] += lax.dot_general(new, new, LANES, precision=HIGH, preferred_element_type=F32)

    def whole_gram(it, copies):
        for copy in copies:
            copy.wait_recv()
        total = grams[it, 0, :, 0:rank]
        for s in range(1, nrow):
            total = total + grams[it, s, :, 0:rank]
        return total

    def update_w(it):
        copies = []
        for s in range(1, nsub):
            theirs = pl.multiple_of(peer("sub", s) * half, half)
            copies.append(
                push(acc.at[it, pl.ds(theirs, half)], subs.at[it, s - 1], sub_send.at[it, s - 1], sub_recv.at[it, s - 1], {"sub": peer("sub", s)})
            )
        mine = pl.ds(pl.multiple_of(sub * half, half), half)
        for copy in copies:
            copy.wait_recv()
        chip = acc[it, mine, :]
        for s in range(1, nsub):
            chip = chip + subs[it, s - 1]
        parts[it, frm, :, 0:rows] = chip[:, :rows].astype(BF16)
        fine = chip[:, rows:]
        coarse = fine.astype(BF16)
        parts[it, frm, :, rows : rows + 128] = coarse
        parts[it, frm, :, rows + 128 : rows + 256] = (fine - coarse.astype(F32)).astype(BF16)
        copies = [
            push(parts.at[it, frm], parts.at[it, frm], part_send.at[it, s - 1], part_recv.at[it, s - 1], {"frm": peer("frm", s)})
            for s in range(1, nfrm)
        ]
        for copy in copies:
            copy.wait_recv()
        total = parts[it, 0].astype(F32)
        for s in range(1, nfrm):
            total = total + parts[it, s].astype(F32)
        gram = total[:, rows : rows + rank] + total[:, rows + 128 : rows + 128 + rank]
        den = jnp.dot(gram, wt[it], precision=HIGH, preferred_element_type=F32)
        wt[it + 1, mine, :] = wt[it, mine, :] * total[:, :rows] / den
        copies = [
            push(wt.at[it + 1, mine], wt.at[it + 1, mine], w_send.at[it, s - 1], w_recv.at[it, s - 1], {"sub": peer("sub", s)})
            for s in range(1, nsub)
        ]
        for copy in copies:
            copy.wait_recv()

    for it in range(ITERS):
        w_low = wt[it].astype(BF16)
        if it:
            gram_copies = share_gram(it)
        waiting = []
        gram = None
        for q in range(CHUNKS):
            if it == 0:
                wavelets(q)
            waiting.append(project(it, q, w_low))
            if it == 0 and q >= 2:
                if gram is None:
                    gram = whole_gram(it, gram_copies)
                update_h(it, q - 2, waiting[q - 2], gram)
        if gram is None:
            gram = whole_gram(it, gram_copies)
        for q in range(CHUNKS - 2 if it == 0 else 0, CHUNKS):
            update_h(it, q, waiting[q], gram)
        update_w(it)
    w_out[...] = wt[ITERS]

    for copy in sent:
        copy.wait_send()

    @pl.when(has_right)
    def _():
        edge(1).wait_send()

    @pl.when(has_left)
    def _():
        edge(-1).wait_send()


def solution(mesh):
    sizes = nfrm, nrow, nsub = tuple(mesh.shape[name] for name in ("frm", "row", "sub"))
    circ = circulants()

    def shards(signal, w_start, h_start):
        channels, frames = signal.shape
        rows, rank = w_start.shape
        half = rank // nsub
        wide = frames // CHUNKS
        w = w_start.reshape(channels, NF, rank).transpose(2, 1, 0).reshape(rank, rows)
        dma = pltpu.SemaphoreType.DMA
        vmem = pl.BlockSpec(memory_space=pltpu.VMEM)
        w, h = pl.pallas_call(
            functools.partial(kernel, sizes),
            out_shape=(
                jax.ShapeDtypeStruct((rank, rows), F32),
                jax.ShapeDtypeStruct((rank, frames), F32),
            ),
            in_specs=[vmem, vmem, vmem, pl.BlockSpec(memory_space=pl.ANY)],
            out_specs=(vmem, vmem),
            scratch_shapes=[
                pltpu.VMEM((NF, TAPS, 2 * TAPS), BF16),
                pltpu.VMEM((NF, 2 * TAPS, 2 * TAPS), BF16),
                pltpu.VMEM((2, channels, TAPS), BF16),
                pltpu.VMEM((frames // TAPS * channels, 2 * TAPS), BF16),
                pltpu.VMEM((rows, frames), BF16),
                pltpu.VMEM((ITERS, nrow, CHUNKS, rank, wide), F32),
                pltpu.VMEM((ITERS, nrow, rank, 128), F32),
                pltpu.VMEM((ITERS, rank, rows + 128), F32),
                pltpu.VMEM((ITERS, nsub - 1, half, rows + 128), F32),
                pltpu.VMEM((ITERS, nfrm, half, rows + 256), BF16),
                pltpu.VMEM((ITERS + 1, rank, rows), F32),
                dma,
                dma((2,)), dma((2,)),
                dma((ITERS, CHUNKS, nrow - 1)), dma((ITERS, CHUNKS, nrow - 1)),
                dma((ITERS, nrow - 1)), dma((ITERS, nrow - 1)),
                dma((ITERS, nsub - 1)), dma((ITERS, nsub - 1)),
                dma((ITERS, nfrm - 1)), dma((ITERS, nfrm - 1)),
                dma((ITERS, nsub - 1)), dma((ITERS, nsub - 1)),
            ],
            compiler_params=pltpu.CompilerParams(
                collective_id=0, has_side_effects=True, vmem_limit_bytes=56 << 20
            ),
        )(signal, w, h_start, jnp.asarray(circ))
        return w.reshape(rank, NF, channels).transpose(2, 1, 0).reshape(rows, rank), h

    return jax.shard_map(
        shards,
        mesh=mesh,
        in_specs=(P("row", ("grp", "frm", "sub")), P("row", None), P(None, ("grp", "frm", "sub"))),
        out_specs=(P(("grp", "row"), None), P(None, ("grp", "frm", "sub"))),
        check_vma=False,
    )
```

```python
import functools
import math

import jax
import jax.numpy as jnp
import numpy as np
from jax import lax
from jax.experimental import pallas as pl
from jax.experimental.pallas import tpu as pltpu
from jax.sharding import PartitionSpec as P

NF = 40
TAPS = 128
ITERS = 2
CHUNKS = 4
UNROLL = 4
HIGH = lax.Precision.HIGHEST
MESH = pl.DeviceIdType.MESH
F32, BF16 = jnp.float32, jnp.bfloat16
LANES = (((1,), (1,)), ((), ()))


def circulants():
    freq = 2.0 * 12.0 ** (np.arange(NF) / (NF - 1))
    sigma = 7.0 / (2.0 * math.pi * freq)
    times = (np.arange(TAPS) - TAPS // 2) / 50.0
    env = np.exp(-(times[None, :] ** 2) / (2.0 * sigma[:, None] ** 2))
    env = env / np.sqrt(np.sum(env * env, axis=1, keepdims=True))
    phase = 2.0 * math.pi * freq[:, None] * times[None, :]
    taps = np.stack([env * np.cos(phase), env * np.sin(phase)], axis=1).astype(np.float32)
    at = np.arange(TAPS)
    table = taps[:, :, (at[:, None] - at[None, :]) % TAPS]
    return table.transpose(0, 2, 1, 3).reshape(NF, TAPS, 2 * TAPS).astype(BF16)


def kernel(
    sizes,
    sig_ref, w_ref, h_ref, circ_ref,
    w_out, h_out,
    circ, table, halo, lhs, spec, ratios, sums, grams, acc, subs, parts, wt,
    circ_sem, halo_send, halo_recv, sum_send, sum_recv, gram_send, gram_recv,
    sub_send, sub_recv, part_send, part_recv, w_send, w_recv,
):
    nfrm, nrow, nsub = sizes
    frm, row, sub = lax.axis_index("frm"), lax.axis_index("row"), lax.axis_index("sub")
    channels, frames = sig_ref.shape
    rank, rows = w_ref.shape
    half = rank // nsub
    blocks = frames // TAPS
    per = blocks // CHUNKS
    wide = frames // CHUNKS
    place = frm * nsub + sub
    has_left, has_right = place > 0, place < nfrm * nsub - 1
    sent = []

    load = pltpu.make_async_copy(circ_ref, circ, circ_sem)
    load.start()

    def peer(name, step):
        size = {"frm": nfrm, "row": nrow, "sub": nsub}[name]
        return lax.rem(lax.axis_index(name) + step, size)

    def neighbour(side):
        at = place + side
        return {"frm": at // nsub, "sub": lax.rem(at, nsub)}

    grams[...] = jnp.zeros_like(grams)
    acc[...] = jnp.zeros_like(acc)
    wt[0] = w_ref[...]

    barrier = pltpu.get_barrier_semaphore()
    for name, size in (("frm", nfrm), ("row", nrow), ("sub", nsub)):
        for step in range(1, size):
            pl.semaphore_signal(barrier, inc=1, device_id={name: peer(name, step)}, device_id_type=MESH)

    @pl.when(has_left)
    def _():
        pl.semaphore_signal(barrier, inc=1, device_id=neighbour(-1), device_id_type=MESH)

    @pl.when(has_right)
    def _():
        pl.semaphore_signal(barrier, inc=1, device_id=neighbour(1), device_id_type=MESH)

    def push(src, dst, send, recv, to):
        copy = pltpu.make_async_remote_copy(
            src_ref=src, dst_ref=dst, send_sem=send, recv_sem=recv, device_id=to, device_id_type=MESH
        )
        copy.start()
        sent.append(copy)
        return copy

    def edge(side):
        return pltpu.make_async_remote_copy(
            src_ref=sig_ref.at[:, pl.ds(frames - TAPS, TAPS)] if side > 0 else sig_ref.at[:, pl.ds(0, TAPS)],
            dst_ref=halo.at[0 if side > 0 else 1],
            send_sem=halo_send.at[0 if side > 0 else 1],
            recv_sem=halo_recv.at[0 if side > 0 else 1],
            device_id=neighbour(side),
            device_id_type=MESH,
        )

    def share_gram(it):
        now = wt[it]
        grams[it, row, :, 0:rank] = lax.dot_general(now, now, LANES, precision=HIGH, preferred_element_type=F32)
        return [
            push(grams.at[it, row], grams.at[it, row], gram_send.at[it, s - 1], gram_recv.at[it, s - 1], {"row": peer("row", s)})
            for s in range(1, nrow)
        ]

    @pl.when(jnp.logical_not(has_left))
    def _():
        halo[0] = jnp.zeros((channels, TAPS), BF16)

    @pl.when(jnp.logical_not(has_right))
    def _():
        halo[1] = jnp.zeros((channels, TAPS), BF16)

    def greet():
        sides = has_left.astype(jnp.int32) + has_right.astype(jnp.int32)
        pl.semaphore_wait(barrier, nfrm + nrow + nsub - 3 + sides)

        @pl.when(has_right)
        def _():
            edge(1).start()

        @pl.when(has_left)
        def _():
            edge(-1).start()

    low_half = lax.broadcasted_iota(jnp.int32, (channels, TAPS), 1) < TAPS // 2

    def turned(block):
        return pltpu.roll(block.astype(F32), TAPS // 2, 1)

    def window(i, before, after):
        piece = jnp.where(low_half, before, after).astype(BF16)
        if i < blocks:
            lhs[i * channels : (i + 1) * channels, 0:TAPS] = piece
        if i > 0:
            lhs[(i - 1) * channels : i * channels, TAPS : 2 * TAPS] = piece

    before = turned(sig_ref[:, 0:TAPS])
    for i in range(1, blocks):
        after = turned(sig_ref[:, i * TAPS : (i + 1) * TAPS])
        window(i, before, after)
        before = after

    def outer_windows():
        @pl.when(has_left)
        def _():
            edge(1).wait_recv()

        @pl.when(has_right)
        def _():
            edge(-1).wait_recv()

        window(0, turned(halo[0]), turned(sig_ref[:, 0:TAPS]))
        window(blocks, turned(sig_ref[:, frames - TAPS : frames]), turned(halo[1]))

    source = lax.broadcasted_iota(jnp.int32, (TAPS, 2 * TAPS), 0)
    target = lax.rem(lax.broadcasted_iota(jnp.int32, (TAPS, 2 * TAPS), 1), TAPS)
    lead = jnp.where(source >= target, 1.0, 0.0).astype(BF16)
    trail = jnp.where(source >= target, 0.0, 1.0).astype(BF16)
    load.wait()

    def fill(f, carry):
        table[f, 0:TAPS, :] = circ[f] * lead
        table[f, TAPS : 2 * TAPS, :] = circ[f] * trail
        return carry

    lax.fori_loop(0, NF, fill, 0)

    def wavelets(q):
        first = q * per

        def group(g, carry):
            for u in range(UNROLL):
                f = g * UNROLL + u
                out = jnp.dot(
                    lhs[first * channels : (first + per) * channels, :], table[f], preferred_element_type=F32
                )
                power = (out[:, :TAPS] * out[:, :TAPS] + out[:, TAPS:] * out[:, TAPS:]).astype(BF16)
                at = pl.multiple_of(f * channels, channels)
                for b in range(per):
                    spec[pl.ds(at, channels), (first + b) * TAPS : (first + b + 1) * TAPS] = power[
                        b * channels : (b + 1) * channels
                    ]
            return carry

        lax.fori_loop(0, NF // UNROLL, group, 0)

    def project(it, q, w_low):
        value = jnp.dot(w_low, spec[:, q * wide : (q + 1) * wide], preferred_element_type=F32)
        coarse = value.astype(BF16)
        sums[it, 0, row, q] = coarse
        sums[it, 1, row, q] = (value - coarse.astype(F32)).astype(BF16)

    def share_sums(it, part, q):
        return [
            push(
                sums.at[it, part, row, q], sums.at[it, part, row, q],
                sum_send.at[it, part, q, s - 1], sum_recv.at[it, part, q, s - 1], {"row": peer("row", s)},
            )
            for s in range(1, nrow)
        ]

    def ratio(it, q, gram):
        cols = slice(q * wide, (q + 1) * wide)
        old = h_ref[:, cols] if it == 0 else h_out[:, cols]
        ratios[:, cols] = old / jnp.dot(gram, old, precision=HIGH, preferred_element_type=F32)

    def update_h(it, q, copies):
        for copy in copies:
            copy.wait_recv()
        total = sums[it, 0, 0, q].astype(F32)
        for s in range(1, nrow):
            total = total + sums[it, 0, s, q].astype(F32)
        cols = slice(q * wide, (q + 1) * wide)
        new = ratios[:, cols] * total
        acc[it, :, 0:rows] += lax.dot_general(new.astype(BF16), spec[:, cols], LANES, preferred_element_type=F32)
        acc[it, :, rows : rows + rank] += lax.dot_general(new, new, LANES, precision=HIGH, preferred_element_type=F32)

    def finish_h(it, q, copies):
        for copy in copies:
            copy.wait_recv()
        total = sums[it, 0, 0, q].astype(F32) + sums[it, 1, 0, q].astype(F32)
        for s in range(1, nrow):
            total = total + (sums[it, 0, s, q].astype(F32) + sums[it, 1, s, q].astype(F32))
        cols = slice(q * wide, (q + 1) * wide)
        h_out[:, cols] = ratios[:, cols] * total

    def whole_gram(it, copies):
        for copy in copies:
            copy.wait_recv()
        total = grams[it, 0, :, 0:rank]
        for s in range(1, nrow):
            total = total + grams[it, s, :, 0:rank]
        return total

    def update_w(it, meanwhile):
        copies = []
        for s in range(1, nsub):
            theirs = pl.multiple_of(peer("sub", s) * half, half)
            copies.append(
                push(acc.at[it, pl.ds(theirs, half)], subs.at[it, s - 1], sub_send.at[it, s - 1], sub_recv.at[it, s - 1], {"sub": peer("sub", s)})
            )
        mine = pl.ds(pl.multiple_of(sub * half, half), half)
        for copy in copies:
            copy.wait_recv()
        chip = acc[it, mine, :]
        for s in range(1, nsub):
            chip = chip + subs[it, s - 1]
        parts[it, frm, :, 0:rows] = chip[:, :rows].astype(BF16)
        fine = chip[:, rows:]
        coarse = fine.astype(BF16).astype(F32)
        parts[it, frm, :, rows:] = (coarse + pltpu.roll(fine - coarse, rank, 1)).astype(BF16)
        copies = [
            push(parts.at[it, frm], parts.at[it, frm], part_send.at[it, s - 1], part_recv.at[it, s - 1], {"frm": peer("frm", s)})
            for s in range(1, nfrm)
        ]
        meanwhile()
        for copy in copies:
            copy.wait_recv()
        total = parts[it, 0].astype(F32)
        for s in range(1, nfrm):
            total = total + parts[it, s].astype(F32)
        gram = (total[:, rows:] + pltpu.roll(total[:, rows:], 128 - rank, 1))[:, :rank]
        den = jnp.dot(gram, wt[it], precision=HIGH, preferred_element_type=F32)
        wt[it + 1, mine, :] = wt[it, mine, :] * total[:, :rows] / den
        copies = [
            push(wt.at[it + 1, mine], wt.at[it + 1, mine], w_send.at[it, s - 1], w_recv.at[it, s - 1], {"sub": peer("sub", s)})
            for s in range(1, nsub)
        ]
        for copy in copies:
            copy.wait_recv()

    order = [*range(1, CHUNKS - 1), 0, CHUNKS - 1]
    for it in range(ITERS):
        w_low = wt[it].astype(BF16)
        leading, trailing = {}, {}
        if it == 0:
            wavelets(order[0])
            greet()
            gram_copies = share_gram(it)
            gram = None
            for k, q in enumerate(order):
                if k:
                    if k == len(order) - 2:
                        outer_windows()
                    wavelets(q)
                project(it, q, w_low)
                leading[q] = share_sums(it, 0, q)
                if k:
                    if gram is None:
                        gram = whole_gram(it, gram_copies)
                    trailing[order[k - 1]] = share_sums(it, 1, order[k - 1])
                    ratio(it, order[k - 1], gram)
                    update_h(it, order[k - 1], leading[order[k - 1]])
            last = order[-1:]
            ratio(it, last[0], gram)
        else:
            gram_copies = share_gram(it)
            for q in order:
                project(it, q, w_low)
                leading[q] = share_sums(it, 0, q)
            gram = whole_gram(it, gram_copies)
            last = order
            for q in order:
                ratio(it, q, gram)
        for q in order:
            if q not in trailing:
                trailing[q] = share_sums(it, 1, q)
        for q in last:
            update_h(it, q, leading[q])

        def meanwhile():
            for q in order:
                finish_h(it, q, trailing[q])

        update_w(it, meanwhile)
    w_out[...] = wt[ITERS]

    for copy in sent:
        copy.wait_send()

    @pl.when(has_right)
    def _():
        edge(1).wait_send()

    @pl.when(has_left)
    def _():
        edge(-1).wait_send()


def solution(mesh):
    sizes = nfrm, nrow, nsub = tuple(mesh.shape[name] for name in ("frm", "row", "sub"))
    circ = circulants()

    def shards(signal, w_start, h_start):
        channels, frames = signal.shape
        rows, rank = w_start.shape
        half = rank // nsub
        wide = frames // CHUNKS
        w = w_start.reshape(channels, NF, rank).transpose(2, 1, 0).reshape(rank, rows)
        dma = pltpu.SemaphoreType.DMA
        vmem = pl.BlockSpec(memory_space=pltpu.VMEM)
        w, h = pl.pallas_call(
            functools.partial(kernel, sizes),
            out_shape=(
                jax.ShapeDtypeStruct((rank, rows), F32),
                jax.ShapeDtypeStruct((rank, frames), F32),
            ),
            in_specs=[vmem, vmem, vmem, pl.BlockSpec(memory_space=pl.ANY)],
            out_specs=(vmem, vmem),
            scratch_shapes=[
                pltpu.VMEM((NF, TAPS, 2 * TAPS), BF16),
                pltpu.VMEM((NF, 2 * TAPS, 2 * TAPS), BF16),
                pltpu.VMEM((2, channels, TAPS), BF16),
                pltpu.VMEM((frames // TAPS * channels, 2 * TAPS), BF16),
                pltpu.VMEM((rows, frames), BF16),
                pltpu.VMEM((rank, frames), F32),
                pltpu.VMEM((ITERS, 2, nrow, CHUNKS, rank, wide), BF16),
                pltpu.VMEM((ITERS, nrow, rank, 128), F32),
                pltpu.VMEM((ITERS, rank, rows + 128), F32),
                pltpu.VMEM((ITERS, nsub - 1, half, rows + 128), F32),
                pltpu.VMEM((ITERS, nfrm, half, rows + 128), BF16),
                pltpu.VMEM((ITERS + 1, rank, rows), F32),
                dma,
                dma((2,)), dma((2,)),
                dma((ITERS, 2, CHUNKS, nrow - 1)), dma((ITERS, 2, CHUNKS, nrow - 1)),
                dma((ITERS, nrow - 1)), dma((ITERS, nrow - 1)),
                dma((ITERS, nsub - 1)), dma((ITERS, nsub - 1)),
                dma((ITERS, nfrm - 1)), dma((ITERS, nfrm - 1)),
                dma((ITERS, nsub - 1)), dma((ITERS, nsub - 1)),
            ],
            compiler_params=pltpu.CompilerParams(
                collective_id=0, has_side_effects=True, vmem_limit_bytes=56 << 20
            ),
        )(signal, w, h_start, jnp.asarray(circ))
        return w.reshape(rank, NF, channels).transpose(2, 1, 0).reshape(rows, rank), h

    return jax.shard_map(
        shards,
        mesh=mesh,
        in_specs=(P("row", ("grp", "frm", "sub")), P("row", None), P(None, ("grp", "frm", "sub"))),
        out_specs=(P(("grp", "row"), None), P(None, ("grp", "frm", "sub"))),
        check_vma=False,
    )
```

```python
import functools
import math

import jax
import jax.numpy as jnp
import numpy as np
from jax import lax
from jax.experimental import pallas as pl
from jax.experimental.pallas import tpu as pltpu
from jax.sharding import PartitionSpec as P

NF = 40
TAPS = 128
ITERS = 2
CHUNKS = 4
UNROLL = 8
MESH = pl.DeviceIdType.MESH
F32, BF16 = jnp.float32, jnp.bfloat16
LANES = (((1,), (1,)), ((), ()))


def circulants():
    freq = 2.0 * 12.0 ** (np.arange(NF) / (NF - 1))
    sigma = 7.0 / (2.0 * math.pi * freq)
    times = (np.arange(TAPS) - TAPS // 2) / 50.0
    env = np.exp(-(times[None, :] ** 2) / (2.0 * sigma[:, None] ** 2))
    env = env / np.sqrt(np.sum(env * env, axis=1, keepdims=True))
    phase = 2.0 * math.pi * freq[:, None] * times[None, :]
    taps = np.stack([env * np.cos(phase), env * np.sin(phase)], axis=1).astype(np.float32)
    at = np.arange(TAPS)
    table = taps[:, :, (at[:, None] - at[None, :]) % TAPS]
    return table.transpose(0, 2, 1, 3).reshape(NF, TAPS, 2 * TAPS).astype(BF16)


def split(value):
    high = value.astype(BF16)
    return high, (value - high.astype(F32)).astype(BF16)


def gram_of(value):
    n = value.shape[0]
    both = jnp.concatenate(split(value), axis=0)
    out = lax.dot_general(both, both, LANES, preferred_element_type=F32)
    return (out[:n, :n] + out[n:, n:]) + (out[:n, n:] + out[n:, :n])


def product(left, right):
    (a, b), (c, d) = split(left), split(right)
    return jnp.dot(
        jnp.concatenate([a, b, a], axis=1), jnp.concatenate([c, c, d], axis=0), preferred_element_type=F32
    )


def kernel(
    sizes,
    sig_ref, w_ref, h_ref, circ_ref,
    w_out, h_out,
    circ, table, halo, lhs, spec, ratios, sums, grams, acc, subs, parts, wt, outer, inner,
    circ_sem, halo_send, halo_recv, sum_send, sum_recv, gram_send, gram_recv,
    sub_send, sub_recv, part_send, part_recv, w_send, w_recv,
):
    nfrm, nrow, nsub = sizes
    frm, row, sub = lax.axis_index("frm"), lax.axis_index("row"), lax.axis_index("sub")
    channels, frames = sig_ref.shape
    rank, rows = w_ref.shape
    half = rank // nsub
    blocks = frames // TAPS
    per = blocks // CHUNKS
    wide = frames // CHUNKS
    place = frm * nsub + sub
    has_left, has_right = place > 0, place < nfrm * nsub - 1
    sent = []

    load = pltpu.make_async_copy(circ_ref, circ, circ_sem)
    load.start()

    def peer(name, step):
        size = {"frm": nfrm, "row": nrow, "sub": nsub}[name]
        return lax.rem(lax.axis_index(name) + step, size)

    def neighbour(side):
        at = place + side
        return {"frm": at // nsub, "sub": lax.rem(at, nsub)}

    grams[...] = jnp.zeros_like(grams)
    acc[...] = jnp.zeros_like(acc)
    outer[...] = w_ref[...].T
    for f in range(NF):
        inner[f * channels : (f + 1) * channels, :] = outer[pl.ds(f, channels, stride=NF), :]
    wt[0] = inner[...].T

    barrier = pltpu.get_barrier_semaphore()
    for name, size in (("frm", nfrm), ("row", nrow), ("sub", nsub)):
        for step in range(1, size):
            pl.semaphore_signal(barrier, inc=1, device_id={name: peer(name, step)}, device_id_type=MESH)

    @pl.when(has_left)
    def _():
        pl.semaphore_signal(barrier, inc=1, device_id=neighbour(-1), device_id_type=MESH)

    @pl.when(has_right)
    def _():
        pl.semaphore_signal(barrier, inc=1, device_id=neighbour(1), device_id_type=MESH)

    def push(src, dst, send, recv, to):
        copy = pltpu.make_async_remote_copy(
            src_ref=src, dst_ref=dst, send_sem=send, recv_sem=recv, device_id=to, device_id_type=MESH
        )
        copy.start()
        sent.append(copy)
        return copy

    def edge(side):
        return pltpu.make_async_remote_copy(
            src_ref=sig_ref.at[:, pl.ds(frames - TAPS, TAPS)] if side > 0 else sig_ref.at[:, pl.ds(0, TAPS)],
            dst_ref=halo.at[0 if side > 0 else 1],
            send_sem=halo_send.at[0 if side > 0 else 1],
            recv_sem=halo_recv.at[0 if side > 0 else 1],
            device_id=neighbour(side),
            device_id_type=MESH,
        )

    def share_gram(it):
        now = wt[it]
        grams[it, row, :, 0:rank] = gram_of(now)
        return [
            push(grams.at[it, row], grams.at[it, row], gram_send.at[it, s - 1], gram_recv.at[it, s - 1], {"row": peer("row", s)})
            for s in range(1, nrow)
        ]

    @pl.when(jnp.logical_not(has_left))
    def _():
        halo[0] = jnp.zeros((channels, TAPS), BF16)

    @pl.when(jnp.logical_not(has_right))
    def _():
        halo[1] = jnp.zeros((channels, TAPS), BF16)

    def greet():
        sides = has_left.astype(jnp.int32) + has_right.astype(jnp.int32)
        pl.semaphore_wait(barrier, nfrm + nrow + nsub - 3 + sides)

        @pl.when(has_right)
        def _():
            edge(1).start()

        @pl.when(has_left)
        def _():
            edge(-1).start()

    low_half = lax.broadcasted_iota(jnp.int32, (channels, TAPS), 1) < TAPS // 2

    def turned(block):
        return pltpu.roll(block.astype(F32), TAPS // 2, 1)

    def window(i, before, after):
        piece = jnp.where(low_half, before, after).astype(BF16)
        if i < blocks:
            lhs[i * channels : (i + 1) * channels, 0:TAPS] = piece
        if i > 0:
            lhs[(i - 1) * channels : i * channels, TAPS : 2 * TAPS] = piece

    before = turned(sig_ref[:, 0:TAPS])
    for i in range(1, blocks):
        after = turned(sig_ref[:, i * TAPS : (i + 1) * TAPS])
        window(i, before, after)
        before = after

    def outer_windows():
        @pl.when(has_left)
        def _():
            edge(1).wait_recv()

        @pl.when(has_right)
        def _():
            edge(-1).wait_recv()

        window(0, turned(halo[0]), turned(sig_ref[:, 0:TAPS]))
        window(blocks, turned(sig_ref[:, frames - TAPS : frames]), turned(halo[1]))

    source = lax.broadcasted_iota(jnp.int32, (TAPS, 2 * TAPS), 0)
    target = lax.rem(lax.broadcasted_iota(jnp.int32, (TAPS, 2 * TAPS), 1), TAPS)
    lead = jnp.where(source >= target, 1.0, 0.0).astype(BF16)
    trail = jnp.where(source >= target, 0.0, 1.0).astype(BF16)
    load.wait()

    def fill(f, carry):
        table[f, 0:TAPS, :] = circ[f] * lead
        table[f, TAPS : 2 * TAPS, :] = circ[f] * trail
        return carry

    lax.fori_loop(0, NF, fill, 0)

    def wavelets(q):
        first = q * per

        def group(g, carry):
            for u in range(UNROLL):
                f = g * UNROLL + u
                out = jnp.dot(
                    lhs[first * channels : (first + per) * channels, :], table[f], preferred_element_type=F32
                )
                power = (out[:, :TAPS] * out[:, :TAPS] + out[:, TAPS:] * out[:, TAPS:]).astype(BF16)
                at = pl.multiple_of(f * channels, channels)
                for b in range(per):
                    spec[pl.ds(at, channels), (first + b) * TAPS : (first + b + 1) * TAPS] = power[
                        b * channels : (b + 1) * channels
                    ]
            return carry

        lax.fori_loop(0, NF // UNROLL, group, 0)

    def project(it, q, w_low):
        value = jnp.dot(w_low, spec[:, q * wide : (q + 1) * wide], preferred_element_type=F32)
        coarse = value.astype(BF16)
        sums[it, 0, row, q] = coarse
        sums[it, 1, row, q] = (value - coarse.astype(F32)).astype(BF16)

    def share_sums(it, part, q):
        return [
            push(
                sums.at[it, part, row, q], sums.at[it, part, row, q],
                sum_send.at[it, part, q, s - 1], sum_recv.at[it, part, q, s - 1], {"row": peer("row", s)},
            )
            for s in range(1, nrow)
        ]

    def ratio(it, q, gram):
        cols = slice(q * wide, (q + 1) * wide)
        old = h_ref[:, cols] if it == 0 else h_out[:, cols]
        ratios[:, cols] = old / product(gram, old)

    def update_h(it, q, copies):
        for copy in copies:
            copy.wait_recv()
        total = sums[it, 0, 0, q].astype(F32)
        for s in range(1, nrow):
            total = total + sums[it, 0, s, q].astype(F32)
        cols = slice(q * wide, (q + 1) * wide)
        new = ratios[:, cols] * total
        acc[it, :, 0:rows] += lax.dot_general(new.astype(BF16), spec[:, cols], LANES, preferred_element_type=F32)
        acc[it, :, rows : rows + rank] += gram_of(new)

    def finish_h(it, q, copies):
        for copy in copies:
            copy.wait_recv()
        total = sums[it, 0, 0, q].astype(F32) + sums[it, 1, 0, q].astype(F32)
        for s in range(1, nrow):
            total = total + (sums[it, 0, s, q].astype(F32) + sums[it, 1, s, q].astype(F32))
        cols = slice(q * wide, (q + 1) * wide)
        h_out[:, cols] = ratios[:, cols] * total

    def whole_gram(it, copies):
        for copy in copies:
            copy.wait_recv()
        total = grams[it, 0, :, 0:rank]
        for s in range(1, nrow):
            total = total + grams[it, s, :, 0:rank]
        return total

    def update_w(it, meanwhile):
        copies = []
        for s in range(1, nsub):
            theirs = pl.multiple_of(peer("sub", s) * half, half)
            copies.append(
                push(acc.at[it, pl.ds(theirs, half)], subs.at[it, s - 1], sub_send.at[it, s - 1], sub_recv.at[it, s - 1], {"sub": peer("sub", s)})
            )
        mine = pl.ds(pl.multiple_of(sub * half, half), half)
        for copy in copies:
            copy.wait_recv()
        chip = acc[it, mine, :]
        for s in range(1, nsub):
            chip = chip + subs[it, s - 1]
        parts[it, frm, :, 0:rows] = chip[:, :rows].astype(BF16)
        fine = chip[:, rows:]
        coarse = fine.astype(BF16).astype(F32)
        parts[it, frm, :, rows:] = (coarse + pltpu.roll(fine - coarse, rank, 1)).astype(BF16)
        copies = [
            push(parts.at[it, frm], parts.at[it, frm], part_send.at[it, s - 1], part_recv.at[it, s - 1], {"frm": peer("frm", s)})
            for s in range(1, nfrm)
        ]
        meanwhile()
        for copy in copies:
            copy.wait_recv()
        total = parts[it, 0].astype(F32)
        for s in range(1, nfrm):
            total = total + parts[it, s].astype(F32)
        gram = (total[:, rows:] + pltpu.roll(total[:, rows:], 128 - rank, 1))[:, :rank]
        den = product(gram, wt[it])
        wt[it + 1, mine, :] = wt[it, mine, :] * total[:, :rows] / den
        copies = [
            push(wt.at[it + 1, mine], wt.at[it + 1, mine], w_send.at[it, s - 1], w_recv.at[it, s - 1], {"sub": peer("sub", s)})
            for s in range(1, nsub)
        ]
        for copy in copies:
            copy.wait_recv()

    order = [*range(1, CHUNKS - 1), 0, CHUNKS - 1]
    for it in range(ITERS):
        w_low = wt[it].astype(BF16)
        leading, trailing = {}, {}
        if it == 0:
            wavelets(order[0])
            greet()
            gram_copies = share_gram(it)
            gram = None
            for k, q in enumerate(order):
                if k:
                    if k == len(order) - 2:
                        outer_windows()
                    wavelets(q)
                project(it, q, w_low)
                leading[q] = share_sums(it, 0, q)
                if k:
                    if gram is None:
                        gram = whole_gram(it, gram_copies)
                    trailing[order[k - 1]] = share_sums(it, 1, order[k - 1])
                    ratio(it, order[k - 1], gram)
                    update_h(it, order[k - 1], leading[order[k - 1]])
            last = order[-1:]
            ratio(it, last[0], gram)
        else:
            gram_copies = share_gram(it)
            for q in order:
                project(it, q, w_low)
                leading[q] = share_sums(it, 0, q)
            gram = whole_gram(it, gram_copies)
            last = order
            for q in order:
                ratio(it, q, gram)
        for q in order:
            if q not in trailing:
                trailing[q] = share_sums(it, 1, q)
        for q in last:
            update_h(it, q, leading[q])

        def meanwhile():
            for q in order:
                finish_h(it, q, trailing[q])

        update_w(it, meanwhile)
    inner[...] = wt[ITERS].T
    for c in range(channels):
        outer[c * NF : (c + 1) * NF, :] = inner[pl.ds(c, NF, stride=channels), :]
    w_out[...] = outer[...].T

    for copy in sent:
        copy.wait_send()

    @pl.when(has_right)
    def _():
        edge(1).wait_send()

    @pl.when(has_left)
    def _():
        edge(-1).wait_send()


def solution(mesh):
    sizes = nfrm, nrow, nsub = tuple(mesh.shape[name] for name in ("frm", "row", "sub"))
    circ = circulants()

    def shards(signal, w_start, h_start):
        channels, frames = signal.shape
        rows, rank = w_start.shape
        half = rank // nsub
        wide = frames // CHUNKS
        dma = pltpu.SemaphoreType.DMA
        vmem = pl.BlockSpec(memory_space=pltpu.VMEM)
        w, h = pl.pallas_call(
            functools.partial(kernel, sizes),
            out_shape=(
                jax.ShapeDtypeStruct((rank, rows), F32),
                jax.ShapeDtypeStruct((rank, frames), F32),
            ),
            in_specs=[vmem, vmem, vmem, pl.BlockSpec(memory_space=pl.ANY)],
            out_specs=(vmem, vmem),
            scratch_shapes=[
                pltpu.VMEM((NF, TAPS, 2 * TAPS), BF16),
                pltpu.VMEM((NF, 2 * TAPS, 2 * TAPS), BF16),
                pltpu.VMEM((2, channels, TAPS), BF16),
                pltpu.VMEM((frames // TAPS * channels, 2 * TAPS), BF16),
                pltpu.VMEM((rows, frames), BF16),
                pltpu.VMEM((rank, frames), F32),
                pltpu.VMEM((ITERS, 2, nrow, CHUNKS, rank, wide), BF16),
                pltpu.VMEM((ITERS, nrow, rank, 128), F32),
                pltpu.VMEM((ITERS, rank, rows + 128), F32),
                pltpu.VMEM((ITERS, nsub - 1, half, rows + 128), F32),
                pltpu.VMEM((ITERS, nfrm, half, rows + 128), BF16),
                pltpu.VMEM((ITERS + 1, rank, rows), F32),
                pltpu.VMEM((rows, rank), F32),
                pltpu.VMEM((rows, rank), F32),
                dma,
                dma((2,)), dma((2,)),
                dma((ITERS, 2, CHUNKS, nrow - 1)), dma((ITERS, 2, CHUNKS, nrow - 1)),
                dma((ITERS, nrow - 1)), dma((ITERS, nrow - 1)),
                dma((ITERS, nsub - 1)), dma((ITERS, nsub - 1)),
                dma((ITERS, nfrm - 1)), dma((ITERS, nfrm - 1)),
                dma((ITERS, nsub - 1)), dma((ITERS, nsub - 1)),
            ],
            compiler_params=pltpu.CompilerParams(
                collective_id=0, has_side_effects=True, vmem_limit_bytes=56 << 20
            ),
        )(signal, w_start.T, h_start, jnp.asarray(circ))
        return w.T, h

    return jax.shard_map(
        shards,
        mesh=mesh,
        in_specs=(P("row", ("grp", "frm", "sub")), P("row", None), P(None, ("grp", "frm", "sub"))),
        out_specs=(P(("grp", "row"), None), P(None, ("grp", "frm", "sub"))),
        check_vma=False,
    )
```

```python
import functools
import math

import jax
import jax.numpy as jnp
import numpy as np
from jax import lax
from jax.experimental import pallas as pl
from jax.experimental.pallas import tpu as pltpu
from jax.sharding import PartitionSpec as P

NF = 40
TAPS = 128
ITERS = 2
CHUNKS = 4
UNROLL = 8
MESH = pl.DeviceIdType.MESH
F32, BF16 = jnp.float32, jnp.bfloat16
LANES = (((1,), (1,)), ((), ()))


def circulants():
    freq = 2.0 * 12.0 ** (np.arange(NF) / (NF - 1))
    sigma = 7.0 / (2.0 * math.pi * freq)
    times = (np.arange(TAPS) - TAPS // 2) / 50.0
    env = np.exp(-(times[None, :] ** 2) / (2.0 * sigma[:, None] ** 2))
    env = env / np.sqrt(np.sum(env * env, axis=1, keepdims=True))
    phase = 2.0 * math.pi * freq[:, None] * times[None, :]
    taps = np.stack([env * np.cos(phase), env * np.sin(phase)], axis=1).astype(np.float32)
    at = np.arange(TAPS)
    table = taps[:, :, (at[:, None] - at[None, :]) % TAPS]
    return table.transpose(0, 2, 1, 3).reshape(NF, TAPS, 2 * TAPS).astype(BF16)


def split(value):
    high = value.astype(BF16)
    return high, (value - high.astype(F32)).astype(BF16)


def gram_of(value):
    n = value.shape[0]
    both = jnp.concatenate(split(value), axis=0)
    out = lax.dot_general(both, both, LANES, preferred_element_type=F32)
    return (out[:n, :n] + out[n:, n:]) + (out[:n, n:] + out[n:, :n])


def product(left, right):
    (a, b), (c, d) = split(left), split(right)
    return jnp.dot(
        jnp.concatenate([a, b, a], axis=1), jnp.concatenate([c, c, d], axis=0), preferred_element_type=F32
    )


def kernel(
    sizes,
    sig_ref, w_ref, h_ref, circ_ref,
    w_out, h_out,
    circ, table, halo, lhs, spec, ratios, sums, grams, acc, subs, parts, wt, outer, inner,
    circ_sem, halo_send, halo_recv, sum_send, sum_recv, gram_send, gram_recv,
    sub_send, sub_recv, part_send, part_recv, w_send, w_recv,
):
    nfrm, nrow, nsub = sizes
    frm, row, sub = lax.axis_index("frm"), lax.axis_index("row"), lax.axis_index("sub")
    channels, frames = sig_ref.shape
    rank, rows = w_ref.shape
    half = rank // nsub
    blocks = frames // TAPS
    per = blocks // CHUNKS
    wide = frames // CHUNKS
    place = frm * nsub + sub
    has_left, has_right = place > 0, place < nfrm * nsub - 1
    sent = []

    load = pltpu.make_async_copy(circ_ref, circ, circ_sem)
    load.start()

    def peer(name, step):
        size = {"frm": nfrm, "row": nrow, "sub": nsub}[name]
        return lax.rem(lax.axis_index(name) + step, size)

    def neighbour(side):
        at = place + side
        return {"frm": at // nsub, "sub": lax.rem(at, nsub)}

    grams[...] = jnp.zeros_like(grams)
    acc[...] = jnp.zeros_like(acc)
    outer[...] = w_ref[...].T
    for f in range(NF):
        inner[f * channels : (f + 1) * channels, :] = outer[pl.ds(f, channels, stride=NF), :]
    wt[0] = inner[...].T

    barrier = pltpu.get_barrier_semaphore()
    for name, size in (("frm", nfrm), ("row", nrow), ("sub", nsub)):
        for step in range(1, size):
            pl.semaphore_signal(barrier, inc=1, device_id={name: peer(name, step)}, device_id_type=MESH)

    @pl.when(has_left)
    def _():
        pl.semaphore_signal(barrier, inc=1, device_id=neighbour(-1), device_id_type=MESH)

    @pl.when(has_right)
    def _():
        pl.semaphore_signal(barrier, inc=1, device_id=neighbour(1), device_id_type=MESH)

    def push(src, dst, send, recv, to):
        copy = pltpu.make_async_remote_copy(
            src_ref=src, dst_ref=dst, send_sem=send, recv_sem=recv, device_id=to, device_id_type=MESH
        )
        copy.start()
        sent.append(copy)
        return copy

    def edge(side):
        return pltpu.make_async_remote_copy(
            src_ref=sig_ref.at[:, pl.ds(frames - TAPS, TAPS)] if side > 0 else sig_ref.at[:, pl.ds(0, TAPS)],
            dst_ref=halo.at[0 if side > 0 else 1],
            send_sem=halo_send.at[0 if side > 0 else 1],
            recv_sem=halo_recv.at[0 if side > 0 else 1],
            device_id=neighbour(side),
            device_id_type=MESH,
        )

    def share_gram(it):
        now = wt[it]
        grams[it, row, :, 0:rank] = gram_of(now)
        return [
            push(grams.at[it, row], grams.at[it, row], gram_send.at[it, s - 1], gram_recv.at[it, s - 1], {"row": peer("row", s)})
            for s in range(1, nrow)
        ]

    @pl.when(jnp.logical_not(has_left))
    def _():
        halo[0] = jnp.zeros((channels, TAPS), BF16)

    @pl.when(jnp.logical_not(has_right))
    def _():
        halo[1] = jnp.zeros((channels, TAPS), BF16)

    def greet():
        sides = has_left.astype(jnp.int32) + has_right.astype(jnp.int32)
        pl.semaphore_wait(barrier, nfrm + nrow + nsub - 3 + sides)

        @pl.when(has_right)
        def _():
            edge(1).start()

        @pl.when(has_left)
        def _():
            edge(-1).start()

    low_half = lax.broadcasted_iota(jnp.int32, (channels, TAPS), 1) < TAPS // 2

    def turned(block):
        return pltpu.roll(block.astype(F32), TAPS // 2, 1)

    def window(i, before, after):
        piece = jnp.where(low_half, before, after).astype(BF16)
        if i < blocks:
            lhs[i * channels : (i + 1) * channels, 0:TAPS] = piece
        if i > 0:
            lhs[(i - 1) * channels : i * channels, TAPS : 2 * TAPS] = piece

    before = turned(sig_ref[:, 0:TAPS])
    for i in range(1, blocks):
        after = turned(sig_ref[:, i * TAPS : (i + 1) * TAPS])
        window(i, before, after)
        before = after

    def outer_windows():
        @pl.when(has_left)
        def _():
            edge(1).wait_recv()

        @pl.when(has_right)
        def _():
            edge(-1).wait_recv()

        window(0, turned(halo[0]), turned(sig_ref[:, 0:TAPS]))
        window(blocks, turned(sig_ref[:, frames - TAPS : frames]), turned(halo[1]))

    source = lax.broadcasted_iota(jnp.int32, (TAPS, 2 * TAPS), 0)
    target = lax.rem(lax.broadcasted_iota(jnp.int32, (TAPS, 2 * TAPS), 1), TAPS)
    lead = jnp.where(source >= target, 1.0, 0.0).astype(BF16)
    trail = jnp.where(source >= target, 0.0, 1.0).astype(BF16)
    load.wait()

    def fill(f, carry):
        table[f, 0:TAPS, :] = circ[f] * lead
        table[f, TAPS : 2 * TAPS, :] = circ[f] * trail
        return carry

    lax.fori_loop(0, NF, fill, 0)

    def wavelets(q):
        first = q * per

        def group(g, carry):
            for u in range(UNROLL):
                f = g * UNROLL + u
                out = jnp.dot(
                    lhs[first * channels : (first + per) * channels, :], table[f], preferred_element_type=F32
                )
                power = (out[:, :TAPS] * out[:, :TAPS] + out[:, TAPS:] * out[:, TAPS:]).astype(BF16)
                at = pl.multiple_of(f * channels, channels)
                for b in range(per):
                    spec[pl.ds(at, channels), (first + b) * TAPS : (first + b + 1) * TAPS] = power[
                        b * channels : (b + 1) * channels
                    ]
            return carry

        lax.fori_loop(0, NF // UNROLL, group, 0)

    def project(it, q, w_low):
        value = jnp.dot(w_low, spec[:, q * wide : (q + 1) * wide], preferred_element_type=F32)
        coarse = value.astype(BF16)
        sums[it, 0, row, q] = coarse
        sums[it, 1, row, q] = (value - coarse.astype(F32)).astype(BF16)

    def share_sums(it, part, q):
        return [
            push(
                sums.at[it, part, row, q], sums.at[it, part, row, q],
                sum_send.at[it, part, q, s - 1], sum_recv.at[it, part, q, s - 1], {"row": peer("row", s)},
            )
            for s in range(1, nrow)
        ]

    def ratio(it, q, gram):
        cols = slice(q * wide, (q + 1) * wide)
        old = h_ref[:, cols] if it == 0 else h_out[:, cols]
        ratios[:, cols] = old / product(gram, old)

    def update_h(it, q, copies):
        for copy in copies:
            copy.wait_recv()
        total = sums[it, 0, 0, q].astype(F32)
        for s in range(1, nrow):
            total = total + sums[it, 0, s, q].astype(F32)
        cols = slice(q * wide, (q + 1) * wide)
        new = ratios[:, cols] * total
        acc[it, :, 0:rows] += lax.dot_general(new.astype(BF16), spec[:, cols], LANES, preferred_element_type=F32)
        acc[it, :, rows : rows + rank] += gram_of(new)

    def finish_h(it, q, copies):
        for copy in copies:
            copy.wait_recv()
        total = sums[it, 0, 0, q].astype(F32) + sums[it, 1, 0, q].astype(F32)
        for s in range(1, nrow):
            total = total + (sums[it, 0, s, q].astype(F32) + sums[it, 1, s, q].astype(F32))
        cols = slice(q * wide, (q + 1) * wide)
        h_out[:, cols] = ratios[:, cols] * total

    def whole_gram(it, copies):
        for copy in copies:
            copy.wait_recv()
        total = grams[it, 0, :, 0:rank]
        for s in range(1, nrow):
            total = total + grams[it, s, :, 0:rank]
        return total

    def update_w(it, meanwhile):
        copies = []
        for s in range(1, nsub):
            theirs = pl.multiple_of(peer("sub", s) * half, half)
            copies.append(
                push(acc.at[it, pl.ds(theirs, half)], subs.at[it, s - 1], sub_send.at[it, s - 1], sub_recv.at[it, s - 1], {"sub": peer("sub", s)})
            )
        mine = pl.ds(pl.multiple_of(sub * half, half), half)
        for copy in copies:
            copy.wait_recv()
        chip = acc[it, mine, :]
        for s in range(1, nsub):
            chip = chip + subs[it, s - 1]
        parts[it, frm, :, 0:rows] = chip[:, :rows].astype(BF16)
        fine = chip[:, rows:]
        coarse = fine.astype(BF16).astype(F32)
        parts[it, frm, :, rows:] = (coarse + pltpu.roll(fine - coarse, rank, 1)).astype(BF16)
        copies = [
            push(parts.at[it, frm], parts.at[it, frm], part_send.at[it, s - 1], part_recv.at[it, s - 1], {"frm": peer("frm", s)})
            for s in range(1, nfrm)
        ]
        meanwhile()
        for copy in copies:
            copy.wait_recv()
        total = parts[it, 0].astype(F32)
        for s in range(1, nfrm):
            total = total + parts[it, s].astype(F32)
        gram = (total[:, rows:] + pltpu.roll(total[:, rows:], 128 - rank, 1))[:, :rank]
        den = product(gram, wt[it])
        wt[it + 1, mine, :] = wt[it, mine, :] * total[:, :rows] / den
        copies = [
            push(wt.at[it + 1, mine], wt.at[it + 1, mine], w_send.at[it, s - 1], w_recv.at[it, s - 1], {"sub": peer("sub", s)})
            for s in range(1, nsub)
        ]
        for copy in copies:
            copy.wait_recv()

    order = [*range(1, CHUNKS - 1), 0, CHUNKS - 1]
    for it in range(ITERS):
        w_low = wt[it].astype(BF16)
        leading, trailing = {}, {}
        if it == 0:
            wavelets(order[0])
            greet()
            gram_copies = share_gram(it)
            gram = None
            for k, q in enumerate(order):
                if k:
                    if k == len(order) - 2:
                        outer_windows()
                    wavelets(q)
                project(it, q, w_low)
                leading[q] = share_sums(it, 0, q)
                if k:
                    if gram is None:
                        gram = whole_gram(it, gram_copies)
                    trailing[order[k - 1]] = share_sums(it, 1, order[k - 1])
                    ratio(it, order[k - 1], gram)
                    update_h(it, order[k - 1], leading[order[k - 1]])
            last = order[-1:]
            ratio(it, last[0], gram)
        else:
            gram_copies = share_gram(it)
            for q in order:
                project(it, q, w_low)
                leading[q] = share_sums(it, 0, q)
            gram = whole_gram(it, gram_copies)
            last = order
            for q in order:
                ratio(it, q, gram)
        for q in order:
            if q not in trailing:
                trailing[q] = share_sums(it, 1, q)
        for q in last:
            update_h(it, q, leading[q])

        def meanwhile():
            for q in order:
                finish_h(it, q, trailing[q])

        update_w(it, meanwhile)
    inner[...] = wt[ITERS].T
    for c in range(channels):
        outer[c * NF : (c + 1) * NF, :] = inner[pl.ds(c, NF, stride=channels), :]
    w_out[...] = outer[...].T

    for copy in sent:
        copy.wait_send()

    @pl.when(has_right)
    def _():
        edge(1).wait_send()

    @pl.when(has_left)
    def _():
        edge(-1).wait_send()


def settle(w_ref, h_ref, w_out, h_out):
    w_out[...] = w_ref[...]
    h_out[...] = h_ref[...]


def solution(mesh):
    sizes = nfrm, nrow, nsub = tuple(mesh.shape[name] for name in ("frm", "row", "sub"))
    circ = circulants()

    def shards(signal, w_start, h_start):
        channels, frames = signal.shape
        rows, rank = w_start.shape
        half = rank // nsub
        wide = frames // CHUNKS
        dma = pltpu.SemaphoreType.DMA
        vmem = pl.BlockSpec(memory_space=pltpu.VMEM)
        w, h = pl.pallas_call(
            functools.partial(kernel, sizes),
            out_shape=(
                jax.ShapeDtypeStruct((rank, rows), F32),
                jax.ShapeDtypeStruct((rank, frames), F32),
            ),
            in_specs=[vmem, vmem, vmem, pl.BlockSpec(memory_space=pl.ANY)],
            out_specs=(vmem, vmem),
            scratch_shapes=[
                pltpu.VMEM((NF, TAPS, 2 * TAPS), BF16),
                pltpu.VMEM((NF, 2 * TAPS, 2 * TAPS), BF16),
                pltpu.VMEM((2, channels, TAPS), BF16),
                pltpu.VMEM((frames // TAPS * channels, 2 * TAPS), BF16),
                pltpu.VMEM((rows, frames), BF16),
                pltpu.VMEM((rank, frames), F32),
                pltpu.VMEM((ITERS, 2, nrow, CHUNKS, rank, wide), BF16),
                pltpu.VMEM((ITERS, nrow, rank, 128), F32),
                pltpu.VMEM((ITERS, rank, rows + 128), F32),
                pltpu.VMEM((ITERS, nsub - 1, half, rows + 128), F32),
                pltpu.VMEM((ITERS, nfrm, half, rows + 128), BF16),
                pltpu.VMEM((ITERS + 1, rank, rows), F32),
                pltpu.VMEM((rows, rank), F32),
                pltpu.VMEM((rows, rank), F32),
                dma,
                dma((2,)), dma((2,)),
                dma((ITERS, 2, CHUNKS, nrow - 1)), dma((ITERS, 2, CHUNKS, nrow - 1)),
                dma((ITERS, nrow - 1)), dma((ITERS, nrow - 1)),
                dma((ITERS, nsub - 1)), dma((ITERS, nsub - 1)),
                dma((ITERS, nfrm - 1)), dma((ITERS, nfrm - 1)),
                dma((ITERS, nsub - 1)), dma((ITERS, nsub - 1)),
            ],
            compiler_params=pltpu.CompilerParams(
                collective_id=0, has_side_effects=True, vmem_limit_bytes=56 << 20
            ),
        )(signal, w_start.T, h_start, jnp.asarray(circ))
        w, h = pl.pallas_call(
            settle,
            out_shape=(jax.ShapeDtypeStruct(w.shape, F32), jax.ShapeDtypeStruct(h.shape, F32)),
            in_specs=[vmem, vmem],
            out_specs=(vmem, vmem),
        )(w, h)
        return w.T, h

    return jax.shard_map(
        shards,
        mesh=mesh,
        in_specs=(P("row", ("grp", "frm", "sub")), P("row", None), P(None, ("grp", "frm", "sub"))),
        out_specs=(P(("grp", "row"), None), P(None, ("grp", "frm", "sub"))),
        check_vma=False,
    )
```
